32 devices in a mesh: groups: 2 (over y), store: 4 (over z), mp: 4 (over x, core).
Axes of the slice: x: 2, y: 2, z: 4, core: 2. Of those that a mesh axis runs over, the one named last changes fastest.
Arguments:
- hidden: bfloat16 [8, 128, 4096], P(('groups', 'store')), parts along dimension 0, may hold values from -6 to 6
- query_weight: bfloat16 [4096, 8192], P('store', 'mp'), may hold values from -0.09375 to 0.09375
- keyvalue_weight: bfloat16 [4096, 2048], P('store', 'mp'), may hold values from -0.09375 to 0.09375
- block_store: bfloat16 [128, 1024, 2048], P('groups', 'store', 'mp'), parts along dimension 0, may hold values from -256 to 256
- block_ids: int32 [8, 4], P('groups'), parts along dimension 0, may hold values from 0 to 63, as said below
- offsets: int32 [8, 4], P('groups'), parts along dimension 0, may hold values from 0 to 3135, as said below
- served: int32 [8], P('groups'), parts along dimension 0, may hold values from 0 to 3, each once
Outputs:
- attended: bfloat16 [8, 128, 8192], P(('groups', 'store'), None, 'mp'), parts along dimension 0
The draws below stay inside these ranges and needn't reach their ends.
There are 2 independent parts, one for each index of `groups`. The reference program is written for one: setup_inputs(seed, part) draws one part's arguments, and reference() takes and returns one part's arrays. A program takes and returns all parts, laid end to end along the dimension named above; an argument that names none is the same for every part. Nothing has to cross between parts.
Inputs may be any that keep to these rules, and one draw needn't show every extreme that they name: `block_ids`: the 4 block ids of one request differ. `offsets`: block c of a request starts at c * 1024 plus 0 to 63.
All inputs are finite; a program needn't handle non-finite values.
Results may differ from the reference program's by a relative error of at most 0.004.
The reference program's roundings to bfloat16 on the way count: a program that leaves them out, or rounds other values in their place, can miss the bound.
Values may be sent and summed in bfloat16 or wider, within the bound.
A program may use at most 128 MiB of HBM per device.

```python
import math
import jax
import jax.numpy as jnp
from jax import lax

D = 4096
QH = 64
KVH = 8
HD = 128
NCH = 4
L = 1024
GAP = 64
NEW = 128
BLOCKS = 64
REQUESTS = 4


def draw_block_store(key, part):
    base = jax.random.normal(key, (BLOCKS, L, KVH, 2, HD), jnp.float32)
    base = jnp.clip(base, -5.0, 5.0)
    return base.reshape(BLOCKS, L, KVH * 2 * HD).astype(jnp.bfloat16)


def draw_block_ids(key, part):

    def one_request(number):
        return jax.random.permutation(jax.random.fold_in(key, number), BLOCKS)[:NCH]
    return jax.vmap(one_request)(jnp.arange(REQUESTS)).astype(jnp.int32)


def draw_offsets(key, part):
    jitter = jax.random.randint(key, (REQUESTS, NCH), 0, GAP)
    return (jnp.arange(NCH, dtype=jnp.int32)[None, :] * L + jitter).astype(jnp.int32)


def levels(own_key, shape, cuts, smallest, high):
    def one(dim, blocks):
        steps = jax.random.uniform(jax.random.fold_in(jax.random.fold_in(own_key, 6), dim), (blocks,), jnp.float32, smallest / len(cuts), high / len(cuts))
        return jnp.repeat(jnp.exp(steps), shape[dim] // blocks).reshape((-1,) + (1,) * (len(shape) - dim - 1))

    factor_of = one(*cuts[0])
    for cut in cuts[1:]:
        factor_of = factor_of * one(*cut)
    return factor_of


def gaussian(rng, extent, spread, reach, split=(), held_as=jnp.bfloat16):
    factor_of = levels(rng, extent, split, -0.22, 0.18) if split else 1.0
    array = jax.random.normal(rng, extent, jnp.float32) * spread * factor_of
    return jnp.minimum(jnp.maximum(array, -reach), reach).astype(held_as)


def setup_inputs(seed: int = 0, part: int = 0) -> dict:
    seeds = jax.random.split(jax.random.key(seed), 8)
    own_keys = jax.random.split(jax.random.fold_in(seeds[7], part), 8)
    return {
        "hidden": gaussian(own_keys[0], (REQUESTS, NEW, D), 1.0, 6.0, ((0, 4),)),
        "query_weight": gaussian(seeds[1], (D, QH * HD), D ** -0.5, 0.09375, ((0, 4), (1, 4))),
        "keyvalue_weight": gaussian(seeds[2], (D, KVH * 2 * HD), D ** -0.5, 0.09375, ((0, 4), (1, 4))),
        "block_store": draw_block_store(jax.random.fold_in(jax.random.fold_in(seeds[7], part), 71), part),
        "block_ids": draw_block_ids(jax.random.fold_in(jax.random.fold_in(seeds[7], part), 71), part),
        "offsets": draw_offsets(jax.random.fold_in(jax.random.fold_in(seeds[7], part), 71), part),
        "served": jax.random.permutation(own_keys[6], REQUESTS).astype(jnp.int32),
    }


def rotary_tables(positions, head_size):
    half_size = head_size // 2
    freq_index = jnp.arange(half_size, dtype=jnp.float32)
    inverse = jnp.exp(freq_index * (-2.0 * math.log(500000.0) / head_size))
    period = jnp.floor(2.0 * math.pi / inverse + 0.5)
    position_f = positions.astype(jnp.float32)[:, None]
    angles = jnp.mod(position_f, period[None, :]) / period[None, :] * (2.0 * math.pi)
    return (jnp.cos(angles), jnp.sin(angles))

def rotate(values, cosine, sine_values):
    half_size = values.shape[-1] // 2
    first_half = values[..., :half_size]
    second_half = values[..., half_size:]
    cos_b = cosine[:, None, :]
    sin_b = sine_values[:, None, :]
    return jnp.concatenate([first_half * cos_b - second_half * sin_b, second_half * cos_b + first_half * sin_b], axis=-1)

def attend(queries, cached_keys, cached_values, new_keys, new_values):
    row_count = queries.shape[0]
    head_count = queries.shape[1]
    sharing = head_count // cached_keys.shape[1]
    scaling = 1.0 / math.sqrt(queries.shape[2])
    causal = jnp.arange(row_count)[:, None] >= jnp.arange(row_count)[None, :]

    def one_head(head_index):
        kv_index = head_index // sharing
        q_one = lax.dynamic_index_in_dim(queries, head_index, 1, keepdims=False)
        k_old = lax.dynamic_index_in_dim(cached_keys, kv_index, 1, keepdims=False)
        v_old = lax.dynamic_index_in_dim(cached_values, kv_index, 1, keepdims=False)
        k_new = lax.dynamic_index_in_dim(new_keys, kv_index, 1, keepdims=False)
        v_new = lax.dynamic_index_in_dim(new_values, kv_index, 1, keepdims=False)
        past_scores = jnp.dot(q_one, k_old.T, preferred_element_type=jnp.float32) * scaling
        own_scores = jnp.dot(q_one, k_new.T, preferred_element_type=jnp.float32) * scaling
        own_scores = jnp.where(causal, own_scores, -jnp.inf)
        row_top = jnp.maximum(lax.optimization_barrier(jnp.max(past_scores, axis=1)), lax.optimization_barrier(jnp.max(own_scores, axis=1)))[:, None]
        w_old = jnp.exp(past_scores - row_top)
        w_new = jnp.exp(own_scores - row_top)
        denominator = lax.optimization_barrier(jnp.sum(w_old, axis=1)) + lax.optimization_barrier(jnp.sum(w_new, axis=1))
        mixed = jnp.dot(w_old.astype(jnp.bfloat16), v_old, preferred_element_type=jnp.float32)
        mixed = mixed + jnp.dot(w_new.astype(jnp.bfloat16), v_new, preferred_element_type=jnp.float32)
        return (mixed / denominator[:, None]).astype(jnp.bfloat16)
    per_head = lax.map(one_head, jnp.arange(head_count, dtype=jnp.int32))
    return jnp.transpose(per_head, (1, 0, 2)).reshape(row_count, head_count * queries.shape[2])

def reference(hidden, query_weight, keyvalue_weight, block_store, block_ids, offsets, served):

    def one_slot(slot_index):
        tokens = hidden[slot_index]
        request = served[slot_index]
        queries = jnp.dot(tokens, query_weight, preferred_element_type=jnp.float32).reshape(NEW, QH, HD)
        fresh_proj = jnp.dot(tokens, keyvalue_weight, preferred_element_type=jnp.float32).reshape(NEW, KVH, 2, HD)
        query_pos = NCH * L + GAP + jnp.arange(NEW, dtype=jnp.int32)
        cos_query, sin_query = rotary_tables(query_pos, HD)
        queries = rotate(queries, cos_query, sin_query).astype(jnp.bfloat16)
        new_keys = rotate(fresh_proj[:, :, 0, :], cos_query, sin_query).astype(jnp.bfloat16)
        new_values = fresh_proj[:, :, 1, :].astype(jnp.bfloat16)
        wanted = block_ids[request]
        page_data = jnp.take(block_store, wanted, axis=0).reshape(NCH * L, KVH, 2, HD)
        key_pos = (offsets[request][:, None] + jnp.arange(L, dtype=jnp.int32)[None, :]).reshape(NCH * L)
        cos_key, sin_key = rotary_tables(key_pos, HD)
        cached_keys = rotate(page_data[:, :, 0, :].astype(jnp.float32), cos_key, sin_key).astype(jnp.bfloat16)
        cached_values = page_data[:, :, 1, :]
        return attend(queries, cached_keys, cached_values, new_keys, new_values)
    return lax.map(one_slot, jnp.arange(REQUESTS, dtype=jnp.int32))
```

```python
import functools
import math

import jax
import jax.numpy as jnp
import numpy as np
from jax import lax
from jax.experimental import pallas as pl
from jax.experimental.pallas import tpu as pltpu
from jax.sharding import PartitionSpec as P

HD = 128
HALF = HD // 2
NCH = 4
L = 1024
GAP = 64
BASE = 500000.0


def periods():
    inverse = np.exp(
        np.arange(HALF, dtype=np.float32) * np.float32(-2.0 * math.log(BASE) / HD)
    ).astype(np.float32)
    return np.floor(np.float32(2.0 * math.pi) / inverse + np.float32(0.5)).astype(np.float64)


def signed_tables(positions):
    period = periods()[None, :]
    angles = np.mod(np.asarray(positions, np.float64)[:, None], period) / period * (2.0 * math.pi)
    cos, sin = np.cos(angles), np.sin(angles)
    return (
        np.concatenate([cos, cos], axis=1).astype(np.float32),
        np.concatenate([-sin, sin], axis=1).astype(np.float32),
    )


def offset_tables(offsets):
    period = jnp.asarray(periods(), jnp.float32)[None, :]
    angles = jnp.mod(offsets.astype(jnp.float32)[:, None], period) / period * (2.0 * math.pi)
    cos, sin = jnp.cos(angles), jnp.sin(angles)
    return jnp.concatenate([cos, cos], axis=1), jnp.concatenate([-sin, sin], axis=1)


def gather_body(slots, ids_ref, served_ref, store_ref, out_ref, sems):
    copies = []
    for s in range(slots):
        request = served_ref[s]
        for c in range(NCH):
            copy = pltpu.make_async_copy(
                store_ref.at[ids_ref[request, c]], out_ref.at[s, c], sems.at[s, c]
            )
            copy.start()
            copies.append(copy)
    for copy in copies:
        copy.wait()


def gather_blocks(block_ids, served, block_store):
    slots = served.shape[0]
    shape = (slots, NCH) + block_store.shape[1:]
    return pl.pallas_call(
        functools.partial(gather_body, slots),
        grid_spec=pltpu.PrefetchScalarGridSpec(
            num_scalar_prefetch=2,
            grid=(1,),
            in_specs=[pl.BlockSpec(memory_space=pl.ANY)],
            out_specs=pl.BlockSpec(memory_space=pl.ANY),
            scratch_shapes=[pltpu.SemaphoreType.DMA((slots, NCH))],
        ),
        out_shape=jax.ShapeDtypeStruct(shape, block_store.dtype),
        name="gather_blocks",
    )(block_ids, served, block_store)


def turn(x, cos, sin):
    return x * cos + pltpu.roll(x, HALF, 1) * sin


def attend_body(
    heads, kv_heads, share, fresh_ref, kv_ref, qc_ref, qs_ref, tc_ref, ts_ref, oc_ref, os_ref,
    out_ref, keys, values, queries, scores
):
    rows = fresh_ref.shape[0]
    shards = L // share
    q_cols = heads * HD
    sharing = heads // kv_heads
    past = NCH * L
    qc, qs = qc_ref[...], qs_ref[...]
    for g in range(kv_heads):
        at = q_cols + g * 2 * HD
        keys[g, past:, :] = turn(fresh_ref[:, at : at + HD], qc, qs).astype(jnp.bfloat16)
        values[g, past:, :] = fresh_ref[:, at + HD : at + 2 * HD].astype(jnp.bfloat16)
    for h in range(heads):
        queries[h * rows : (h + 1) * rows, :] = turn(
            fresh_ref[:, h * HD : (h + 1) * HD], qc, qs
        ).astype(jnp.bfloat16)

    def rotate_share(i, carry):
        source = i // NCH
        c = i % NCH
        at_t = pl.multiple_of(source * share, share)
        at_k = pl.multiple_of(i * share, share)
        tc, ts = tc_ref[pl.ds(at_t, share), :], ts_ref[pl.ds(at_t, share), :]
        oc, os = oc_ref[pl.ds(c, 1), :], os_ref[pl.ds(c, 1), :]
        cos = tc * oc - ts * os
        sin = ts * oc + tc * os
        for g in range(kv_heads):
            at = g * 2 * HD
            x = kv_ref[source, c, :, at : at + HD].astype(jnp.float32)
            keys[g, pl.ds(at_k, share), :] = turn(x, cos, sin).astype(jnp.bfloat16)
            values[g, pl.ds(at_k, share), :] = kv_ref[source, c, :, at + HD : at + 2 * HD]
        return carry

    lax.fori_loop(0, shards * NCH, rotate_share, 0)

    block = 2 * rows
    steps = heads // 2
    width = 512
    factor = math.log2(math.e) / math.sqrt(HD)
    lower = lax.broadcasted_iota(jnp.int32, (block, rows), 0) % rows >= lax.broadcasted_iota(
        jnp.int32, (block, rows), 1
    )
    contract = (((1,), (1,)), ((), ()))

    def one_block(b, carry):
        g = (b * 2) // sharing
        q = queries[pl.ds(pl.multiple_of(b * block, block), block), :]
        own = lax.dot_general(q, keys[g, past:, :], contract, preferred_element_type=jnp.float32)
        own = jnp.where(lower, own, -jnp.inf)
        top = own
        for j in range(past // width):
            s = lax.dot_general(
                q, keys[g, j * width : (j + 1) * width, :], contract,
                preferred_element_type=jnp.float32,
            )
            scores[:, j * width : (j + 1) * width] = s
            for k in range(width // HD):
                top = jnp.maximum(top, s[:, k * HD : (k + 1) * HD])
        top = jnp.max(top, axis=1, keepdims=True)
        w = jnp.exp2((own - top) * factor)
        total = w
        mixed = jnp.dot(
            w.astype(jnp.bfloat16), values[g, past:, :], preferred_element_type=jnp.float32
        )
        for j in range(past // width):
            w = jnp.exp2((scores[:, j * width : (j + 1) * width] - top) * factor)
            for k in range(width // HD):
                total = total + w[:, k * HD : (k + 1) * HD]
            mixed = mixed + jnp.dot(
                w.astype(jnp.bfloat16), values[g, j * width : (j + 1) * width, :],
                preferred_element_type=jnp.float32,
            )
        done = (mixed / jnp.sum(total, axis=1, keepdims=True)).astype(out_ref.dtype)
        for k in range(2):
            at = pl.multiple_of((b * 2 + k) * HD, HD)
            out_ref[0, :, pl.ds(at, HD)] = done[k * rows : (k + 1) * rows, :]
        return carry

    lax.fori_loop(0, steps, one_block, 0)


def per_device(hidden, query_weight, keyvalue_weight, block_store, block_ids, offsets, served):
    slots = lax.axis_size("store")
    me = lax.axis_index("store")
    rows, width = hidden.shape[1:]
    share = block_store.shape[1]
    heads = query_weight.shape[1] // HD
    kv_heads = keyvalue_weight.shape[1] // (2 * HD)
    sending = gather_blocks(block_ids, served, block_store)
    received = lax.all_to_all(sending, "store", split_axis=0, concat_axis=0, tiled=True)
    pieces = hidden[0].reshape(rows, slots, width // slots).transpose(1, 0, 2)
    tokens = lax.all_to_all(pieces, "store", split_axis=0, concat_axis=0, tiled=True)
    tokens = tokens.reshape(slots * rows, width // slots)
    partial = jnp.concatenate(
        [
            jnp.dot(tokens, query_weight, preferred_element_type=jnp.float32),
            jnp.dot(tokens, keyvalue_weight, preferred_element_type=jnp.float32),
        ],
        axis=1,
    )
    fresh = lax.psum_scatter(partial, "store", scatter_dimension=0, tiled=True)
    qc, qs = signed_tables(NCH * L + GAP + np.arange(rows))
    tc, ts = signed_tables(np.arange(L))
    oc, os = offset_tables(offsets[served[me]])
    past = NCH * L
    return pl.pallas_call(
        functools.partial(attend_body, heads, kv_heads, share),
        out_shape=jax.ShapeDtypeStruct((1, rows, heads * HD), jnp.bfloat16),
        in_specs=[pl.BlockSpec(memory_space=pltpu.VMEM)] * 8,
        out_specs=pl.BlockSpec(memory_space=pltpu.VMEM),
        scratch_shapes=[
            pltpu.VMEM((kv_heads, past + rows, HD), jnp.bfloat16),
            pltpu.VMEM((kv_heads, past + rows, HD), jnp.bfloat16),
            pltpu.VMEM((heads * rows, HD), jnp.bfloat16),
            pltpu.VMEM((2 * rows, past), jnp.float32),
        ],
        compiler_params=pltpu.CompilerParams(vmem_limit_bytes=48 << 20),
        name="attend",
    )(fresh, received, qc, qs, tc, ts, oc, os)


def solution(mesh):
    in_specs = (
        P(("groups", "store"), None, None),
        P("store", "mp"),
        P("store", "mp"),
        P("groups", "store", "mp"),
        P("groups", None),
        P("groups", None),
        P("groups"),
    )
    out_specs = P(("groups", "store"), None, "mp")
    return jax.shard_map(
        per_device, mesh=mesh, in_specs=in_specs, out_specs=out_specs, check_vma=False
    )
```

```python
import functools
import math

import jax
import jax.numpy as jnp
import numpy as np
from jax import lax
from jax.experimental import pallas as pl
from jax.experimental.pallas import tpu as pltpu
from jax.sharding import PartitionSpec as P

HD = 128
HALF = HD // 2
NCH = 4
L = 1024
GAP = 64
BASE = 500000.0


def periods():
    inverse = np.exp(
        np.arange(HALF, dtype=np.float32) * np.float32(-2.0 * math.log(BASE) / HD)
    ).astype(np.float32)
    return np.floor(np.float32(2.0 * math.pi) / inverse + np.float32(0.5)).astype(np.float64)


def signed_tables(positions):
    period = periods()[None, :]
    angles = np.mod(np.asarray(positions, np.float64)[:, None], period) / period * (2.0 * math.pi)
    cos, sin = np.cos(angles), np.sin(angles)
    return (
        np.concatenate([cos, cos], axis=1).astype(np.float32),
        np.concatenate([-sin, sin], axis=1).astype(np.float32),
    )


def offset_tables(offsets):
    period = jnp.asarray(periods(), jnp.float32)[None, :]
    angles = jnp.mod(offsets.astype(jnp.float32)[:, None], period) / period * (2.0 * math.pi)
    cos, sin = jnp.cos(angles), jnp.sin(angles)
    return jnp.concatenate([cos, cos], axis=1), jnp.concatenate([-sin, sin], axis=1)


def gather_body(ids_ref, served_ref, store_ref, out_ref):
    out_ref[0] = store_ref[...]


def gather_blocks(block_ids, served, block_store):
    slots = served.shape[0]
    block = (1,) + block_store.shape[1:]
    return pl.pallas_call(
        gather_body,
        grid_spec=pltpu.PrefetchScalarGridSpec(
            num_scalar_prefetch=2,
            grid=(slots, NCH),
            in_specs=[pl.BlockSpec(block, lambda s, c, ids, served: (ids[served[s], c], 0, 0))],
            out_specs=pl.BlockSpec((1,) + block, lambda s, c, ids, served: (s, c, 0, 0)),
        ),
        out_shape=jax.ShapeDtypeStruct((slots, NCH) + block_store.shape[1:], block_store.dtype),
        name="gather_blocks",
    )(block_ids, served, block_store)


def turn(x, cos, sin):
    return x * cos + pltpu.roll(x, HALF, 1) * sin


MESH = pl.DeviceIdType.MESH


def serve_body(
    slots, peers, heads, kv_heads,
    hidden_ref, wq_hbm, wkv_hbm, sending_ref, qc_ref, qs_ref, tc_ref, ts_ref, oc_ref, os_ref,
    out_ref,
    tokens, wq, wkv, sums, arrived, blocks, keys, values, queries, scores,
    load_sem, own_sem, a_send, a_recv, b_send, b_recv, k_send, k_recv, p_send, p_recv,
):
    me = lax.axis_index("store")
    part = lax.axis_index("mp")
    rows = hidden_ref.shape[1]
    depth = tokens.shape[2]
    chunks, _, _, width = sums.shape
    share = blocks.shape[2]
    sharing = heads // kv_heads
    past = NCH * L
    strip = rows // peers

    loads = [
        pltpu.make_async_copy(wq_hbm, wq, load_sem.at[0]),
        pltpu.make_async_copy(wkv_hbm, wkv, load_sem.at[1]),
    ]
    for load in loads:
        load.start()
    own_copy = pltpu.make_async_copy(sending_ref.at[me], blocks.at[me], own_sem.at[0])
    own_copy.start()

    barrier = pltpu.get_barrier_semaphore()
    for k in range(1, slots):
        pl.semaphore_signal(
            barrier, inc=1, device_id={"store": lax.rem(me + k, slots)}, device_id_type=MESH
        )
    for k in range(1, peers):
        pl.semaphore_signal(
            barrier, inc=1, device_id={"mp": lax.rem(part + k, peers)}, device_id_type=MESH
        )
    pl.semaphore_wait(barrier, slots + peers - 2)

    def strip_copy(k):
        to = lax.rem(me + k, slots)
        mine = pl.ds(pl.multiple_of(part * strip, strip), strip)
        return pltpu.make_async_remote_copy(
            src_ref=hidden_ref.at[0, mine, pl.ds(pl.multiple_of(to * depth, depth), depth)],
            dst_ref=tokens.at[me, mine, :],
            send_sem=a_send.at[k],
            recv_sem=a_recv.at[k],
            device_id={"store": to},
            device_id_type=MESH,
        )

    def spread_copy(k, d):
        source = lax.rem(me - k + slots, slots)
        mine = pl.ds(pl.multiple_of(part * strip, strip), strip)
        return pltpu.make_async_remote_copy(
            src_ref=tokens.at[source, mine, :],
            dst_ref=tokens.at[source, mine, :],
            send_sem=b_send.at[k, d],
            recv_sem=b_recv.at[k, d],
            device_id={"mp": lax.rem(part + d, peers)},
            device_id_type=MESH,
        )

    def block_copy(k):
        to = lax.rem(me + k, slots)
        return pltpu.make_async_remote_copy(
            src_ref=sending_ref.at[to],
            dst_ref=blocks.at[me],
            send_sem=k_send.at[k],
            recv_sem=k_recv.at[k],
            device_id={"store": to},
            device_id_type=MESH,
        )

    def sum_copy(s, q, up):
        index = s + 1 if up else s
        return pltpu.make_async_remote_copy(
            src_ref=sums.at[q, s],
            dst_ref=arrived.at[index, q],
            send_sem=p_send.at[index, q],
            recv_sem=p_recv.at[index, q],
            device_id={"store": lax.rem(me + 1, slots) if up else lax.rem(me + slots - 1, slots)},
            device_id_type=MESH,
        )

    def each(count, body, first=0):
        def step(i, carry):
            body(i)
            return carry

        lax.fori_loop(first, count, step, 0)

    each(slots, lambda k: strip_copy(k).start(), 1)
    each(slots, lambda k: block_copy(k).start(), 1)
    tokens[me] = hidden_ref[0, :, pl.ds(pl.multiple_of(me * depth, depth), depth)]

    def spread(k):
        strip_copy(k).wait_recv()
        for d in range(1, peers):
            spread_copy(k, d).start()

    each(slots, spread, 1)

    def spread_wait(k):
        for d in range(1, peers):
            spread_copy(k, d).wait_recv()

    each(slots, spread_wait, 1)
    for load in loads:
        load.wait()

    group = 4 if slots % 4 == 0 else 1

    def project(q, panel):
        def some(i):
            t = tokens[pl.ds(i * group, group)].reshape(group * rows, depth)
            sums[q, pl.ds(i * group, group)] = jnp.dot(
                t, panel, preferred_element_type=jnp.float32
            ).reshape(group, rows, width)

        each(slots // group, some)

    def relay_up(k, q):
        s = slots - 1 - k

        @pl.when(s > me)
        def _():
            @pl.when(me > 0)
            def _():
                sum_copy(s, q, True).wait_recv()
                sums[q, s] = sums[q, s] + arrived[s + 1, q]

            sum_copy(s, q, True).start()

    def relay_down(k, q):
        @pl.when(k < me)
        def _():
            @pl.when(me < slots - 1)
            def _():
                sum_copy(k, q, False).wait_recv()
                sums[q, k] = sums[q, k] + arrived[k, q]

            sum_copy(k, q, False).start()

    for q in range(chunks):
        if q < chunks - 1:
            project(q, wq[:, q * width : (q + 1) * width])
        else:
            project(q, wkv[...])

    def relay(i):
        k, q = i // chunks, i % chunks
        relay_up(k, q)
        relay_down(k, q)

    each((slots - 1) * chunks, relay)

    def settle(q):
        @pl.when(me > 0)
        def _():
            sum_copy(me, q, True).wait_recv()
            sums[q, me] = sums[q, me] + arrived[me + 1, q]

        @pl.when(me < slots - 1)
        def _():
            sum_copy(me, q, False).wait_recv()
            sums[q, me] = sums[q, me] + arrived[me, q]

    each(chunks, settle)

    qc, qs = qc_ref[...], qs_ref[...]
    for g in range(kv_heads):
        at = g * 2 * HD
        keys[g, past:, :] = turn(sums[chunks - 1, me, :, at : at + HD], qc, qs).astype(jnp.bfloat16)
        values[g, past:, :] = sums[chunks - 1, me, :, at + HD : at + 2 * HD].astype(jnp.bfloat16)
    for h in range(heads):
        q, at = divmod(h * HD, width)
        queries[h * rows : (h + 1) * rows, :] = turn(
            sums[q, me, :, at : at + HD], qc, qs
        ).astype(jnp.bfloat16)

    def rotate_share(source):
        at_t = pl.multiple_of(source * share, share)
        tc, ts = tc_ref[pl.ds(at_t, share), :], ts_ref[pl.ds(at_t, share), :]

        def one(c):
            at_k = pl.multiple_of((source * NCH + c) * share, share)
            oc, os = oc_ref[pl.ds(c, 1), :], os_ref[pl.ds(c, 1), :]
            cos = tc * oc - ts * os
            sin = ts * oc + tc * os
            for g in range(kv_heads):
                at = g * 2 * HD
                x = blocks[source, c, :, at : at + HD].astype(jnp.float32)
                keys[g, pl.ds(at_k, share), :] = turn(x, cos, sin).astype(jnp.bfloat16)
                values[g, pl.ds(at_k, share), :] = blocks[source, c, :, at + HD : at + 2 * HD]

        each(NCH, one)

    own_copy.wait()
    rotate_share(me)

    def take(k):
        block_copy(k).wait_recv()
        rotate_share(lax.rem(me - k + slots, slots))

    each(slots, take, 1)

    block = 2 * rows
    steps = heads // 2
    span = 512
    factor = math.log2(math.e) / math.sqrt(HD)
    lower = lax.broadcasted_iota(jnp.int32, (block, rows), 0) % rows >= lax.broadcasted_iota(
        jnp.int32, (block, rows), 1
    )
    contract = (((1,), (1,)), ((), ()))

    def one_block(b):
        g = (b * 2) // sharing
        q = queries[pl.ds(pl.multiple_of(b * block, block), block), :]
        own = lax.dot_general(q, keys[g, past:, :], contract, preferred_element_type=jnp.float32)
        own = jnp.where(lower, own, -jnp.inf)
        top = own
        for j in range(past // span):
            s = lax.dot_general(
                q, keys[g, j * span : (j + 1) * span, :], contract,
                preferred_element_type=jnp.float32,
            )
            scores[:, j * span : (j + 1) * span] = s
            for k in range(span // HD):
                top = jnp.maximum(top, s[:, k * HD : (k + 1) * HD])
        top = jnp.max(top, axis=1, keepdims=True)
        w = jnp.exp2((own - top) * factor)
        total = w
        mixed = jnp.dot(
            w.astype(jnp.bfloat16), values[g, past:, :], preferred_element_type=jnp.float32
        )
        for j in range(past // span):
            w = jnp.exp2((scores[:, j * span : (j + 1) * span] - top) * factor)
            for k in range(span // HD):
                total = total + w[:, k * HD : (k + 1) * HD]
            mixed = mixed + jnp.dot(
                w.astype(jnp.bfloat16), values[g, j * span : (j + 1) * span, :],
                preferred_element_type=jnp.float32,
            )
        done = (mixed / jnp.sum(total, axis=1, keepdims=True)).astype(out_ref.dtype)
        for k in range(2):
            at = pl.multiple_of((b * 2 + k) * HD, HD)
            out_ref[0, :, pl.ds(at, HD)] = done[k * rows : (k + 1) * rows, :]

    each(steps, one_block)

    def drain(k):
        strip_copy(k).wait_send()
        block_copy(k).wait_send()
        for d in range(1, peers):
            spread_copy(k, d).wait_send()

    each(slots, drain, 1)

    def drain_sums(i):
        k, q = i // chunks, i % chunks

        @pl.when(slots - 1 - k > me)
        def _():
            sum_copy(slots - 1 - k, q, True).wait_send()

        @pl.when(k < me)
        def _():
            sum_copy(k, q, False).wait_send()

    each((slots - 1) * chunks, drain_sums)


def per_device(hidden, query_weight, keyvalue_weight, block_store, block_ids, offsets, served):
    slots = lax.axis_size("store")
    peers = lax.axis_size("mp")
    me = lax.axis_index("store")
    rows, model = hidden.shape[1:]
    share, kv_cols = block_store.shape[1:]
    q_cols = query_weight.shape[1]
    heads = q_cols // HD
    kv_heads = kv_cols // (2 * HD)
    chunks = q_cols // kv_cols + 1
    depth = model // slots
    past = NCH * L
    sending = gather_blocks(block_ids, served, block_store)
    qc, qs = signed_tables(past + GAP + np.arange(rows))
    tc, ts = signed_tables(np.arange(L))
    oc, os = offset_tables(offsets[served[me]])
    vmem = pl.BlockSpec(memory_space=pltpu.VMEM)
    hbm = pl.BlockSpec(memory_space=pl.ANY)
    dma = pltpu.SemaphoreType.DMA
    return pl.pallas_call(
        functools.partial(serve_body, slots, peers, heads, kv_heads),
        out_shape=jax.ShapeDtypeStruct((1, rows, q_cols), jnp.bfloat16),
        in_specs=[vmem, hbm, hbm, hbm] + [vmem] * 6,
        out_specs=vmem,
        scratch_shapes=[
            pltpu.VMEM((slots, rows, depth), jnp.bfloat16),
            pltpu.VMEM(query_weight.shape, jnp.bfloat16),
            pltpu.VMEM(keyvalue_weight.shape, jnp.bfloat16),
            pltpu.VMEM((chunks, slots, rows, kv_cols), jnp.float32),
            pltpu.VMEM((slots + 1, chunks, rows, kv_cols), jnp.float32),
            pltpu.VMEM((slots, NCH, share, kv_cols), jnp.bfloat16),
            pltpu.VMEM((kv_heads, past + rows, HD), jnp.bfloat16),
            pltpu.VMEM((kv_heads, past + rows, HD), jnp.bfloat16),
            pltpu.VMEM((heads * rows, HD), jnp.bfloat16),
            pltpu.VMEM((2 * rows, past), jnp.float32),
            dma((2,)),
            dma((1,)),
            dma((slots,)),
            dma((slots,)),
            dma((slots, peers)),
            dma((slots, peers)),
            dma((slots,)),
            dma((slots,)),
            dma((slots + 1, chunks)),
            dma((slots + 1, chunks)),
        ],
        compiler_params=pltpu.CompilerParams(
            vmem_limit_bytes=60 << 20, collective_id=0, has_side_effects=True
        ),
        name="serve",
    )(hidden, query_weight, keyvalue_weight, sending, qc, qs, tc, ts, oc, os)


def solution(mesh):
    in_specs = (
        P(("groups", "store"), None, None),
        P("store", "mp"),
        P("store", "mp"),
        P("groups", "store", "mp"),
        P("groups", None),
        P("groups", None),
        P("groups"),
    )
    out_specs = P(("groups", "store"), None, "mp")
    return jax.shard_map(
        per_device, mesh=mesh, in_specs=in_specs, out_specs=out_specs, check_vma=False
    )
```

```python
import functools
import math

import jax
import jax.numpy as jnp
import numpy as np
from jax import lax
from jax.experimental import pallas as pl
from jax.experimental.pallas import tpu as pltpu
from jax.sharding import PartitionSpec as P

HD = 128
HALF = HD // 2
NCH = 4
L = 1024
GAP = 64
BASE = 500000.0


def periods():
    inverse = np.exp(
        np.arange(HALF, dtype=np.float32) * np.float32(-2.0 * math.log(BASE) / HD)
    ).astype(np.float32)
    return np.floor(np.float32(2.0 * math.pi) / inverse + np.float32(0.5)).astype(np.float64)


def signed_tables(positions):
    period = periods()[None, :]
    angles = np.mod(np.asarray(positions, np.float64)[:, None], period) / period * (2.0 * math.pi)
    cos, sin = np.cos(angles), np.sin(angles)
    return (
        np.concatenate([cos, cos], axis=1).astype(np.float32),
        np.concatenate([-sin, sin], axis=1).astype(np.float32),
    )


def offset_tables(offsets):
    period = jnp.asarray(periods(), jnp.float32)[None, :]
    angles = jnp.mod(offsets.astype(jnp.float32)[:, None], period) / period * (2.0 * math.pi)
    cos, sin = jnp.cos(angles), jnp.sin(angles)
    return jnp.concatenate([cos, cos], axis=1), jnp.concatenate([-sin, sin], axis=1)


def gather_body(slots, ids_ref, served_ref, store_ref, out_ref, sems):
    copies = []
    for s in range(slots):
        request = served_ref[s]
        for c in range(NCH):
            copy = pltpu.make_async_copy(
                store_ref.at[ids_ref[request, c]], out_ref.at[s, c], sems.at[s, c]
            )
            copy.start()
            copies.append(copy)
    for copy in copies:
        copy.wait()


def gather_blocks(block_ids, served, block_store):
    slots = served.shape[0]
    return pl.pallas_call(
        functools.partial(gather_body, slots),
        grid_spec=pltpu.PrefetchScalarGridSpec(
            num_scalar_prefetch=2,
            grid=(),
            in_specs=[pl.BlockSpec(memory_space=pl.ANY)],
            out_specs=pl.BlockSpec(memory_space=pltpu.VMEM),
            scratch_shapes=[pltpu.SemaphoreType.DMA((slots, NCH))],
        ),
        out_shape=jax.ShapeDtypeStruct((slots, NCH) + block_store.shape[1:], block_store.dtype),
        compiler_params=pltpu.CompilerParams(vmem_limit_bytes=16 << 20),
        name="gather_blocks",
    )(block_ids, served, block_store)


def turn(x, cos, sin):
    return x * cos + pltpu.roll(x, HALF, 1) * sin


MESH = pl.DeviceIdType.MESH


def serve_body(
    slots, peers, heads, kv_heads,
    hidden_ref, wq_hbm, wkv_hbm, sending_ref, qc_ref, qs_ref, tc_ref, ts_ref, oc_ref, os_ref,
    out_ref,
    tokens, wq, wkv, sums, arrived, blocks, keys, fresh, queries, scores, weights, totals, mixed,
    load_sem, own_sem, a_send, a_recv, b_send, b_recv, k_send, k_recv, p_send, p_recv,
):
    me = lax.axis_index("store")
    part = lax.axis_index("mp")
    rows = hidden_ref.shape[1]
    depth = tokens.shape[2]
    chunks, _, _, width = sums.shape
    share = blocks.shape[2]
    sharing = heads // kv_heads
    past = NCH * L
    strip = rows // peers

    loads = [
        pltpu.make_async_copy(wq_hbm, wq, load_sem.at[0]),
        pltpu.make_async_copy(wkv_hbm, wkv, load_sem.at[1]),
    ]
    for load in loads:
        load.start()
    own_copy = pltpu.make_async_copy(sending_ref.at[me], blocks.at[me], own_sem.at[0])
    own_copy.start()

    barrier = pltpu.get_barrier_semaphore()
    for k in range(1, slots):
        pl.semaphore_signal(
            barrier, inc=1, device_id={"store": lax.rem(me + k, slots)}, device_id_type=MESH
        )
    for k in range(1, peers):
        pl.semaphore_signal(
            barrier, inc=1, device_id={"mp": lax.rem(part + k, peers)}, device_id_type=MESH
        )
    pl.semaphore_wait(barrier, slots + peers - 2)

    def strip_copy(k):
        to = lax.rem(me + k, slots)
        mine = pl.ds(pl.multiple_of(part * strip, strip), strip)
        return pltpu.make_async_remote_copy(
            src_ref=hidden_ref.at[0, mine, pl.ds(pl.multiple_of(to * depth, depth), depth)],
            dst_ref=tokens.at[me, mine, :],
            send_sem=a_send.at[k],
            recv_sem=a_recv.at[k],
            device_id={"store": to},
            device_id_type=MESH,
        )

    def spread_copy(k, d):
        source = lax.rem(me - k + slots, slots)
        mine = pl.ds(pl.multiple_of(part * strip, strip), strip)
        return pltpu.make_async_remote_copy(
            src_ref=tokens.at[source, mine, :],
            dst_ref=tokens.at[source, mine, :],
            send_sem=b_send.at[k, d],
            recv_sem=b_recv.at[k, d],
            device_id={"mp": lax.rem(part + d, peers)},
            device_id_type=MESH,
        )

    def block_copy(k, g, v):
        to = lax.rem(me + k, slots)
        cols = pl.ds(pl.multiple_of((2 * g + v) * HD, HD), HD)
        return pltpu.make_async_remote_copy(
            src_ref=sending_ref.at[to, :, :, cols],
            dst_ref=blocks.at[me, :, :, cols],
            send_sem=k_send.at[k, 2 * g + v],
            recv_sem=k_recv.at[k, 2 * g + v],
            device_id={"store": to},
            device_id_type=MESH,
        )

    half_pieces = (slots - 1) * kv_heads

    def piece(i):
        v, r = i // half_pieces, i % half_pieces
        return block_copy(1 + r // kv_heads, r % kv_heads, v)

    edge = (me == 0) | (me == slots - 1)

    def sum_copy(s, q, up):
        index = s + 1 if up else s
        return pltpu.make_async_remote_copy(
            src_ref=sums.at[q, s],
            dst_ref=arrived.at[index, q],
            send_sem=p_send.at[index, q],
            recv_sem=p_recv.at[index, q],
            device_id={"store": lax.rem(me + 1, slots) if up else lax.rem(me + slots - 1, slots)},
            device_id_type=MESH,
        )

    def each(count, body, first=0):
        def step(i, carry):
            body(i)
            return carry

        lax.fori_loop(first, count, step, 0)

    each(slots, lambda k: strip_copy(k).start(), 1)
    tokens[me] = hidden_ref[0, :, pl.ds(pl.multiple_of(me * depth, depth), depth)]

    def spread(k):
        strip_copy(k).wait_recv()
        for d in range(1, peers):
            spread_copy(k, d).start()

    each(slots, spread, 1)

    def spread_wait(k):
        for d in range(1, peers):
            spread_copy(k, d).wait_recv()

    each(slots, spread_wait, 1)
    for load in loads:
        load.wait()

    group = 4 if slots % 4 == 0 else 1

    def project(q, panel):
        def some(i):
            t = tokens[pl.ds(i * group, group)].reshape(group * rows, depth)
            sums[q, pl.ds(i * group, group)] = jnp.dot(
                t, panel, preferred_element_type=jnp.float32
            ).reshape(group, rows, width)

        each(slots // group, some)

    def relay_up(k, q):
        s = slots - 1 - k

        @pl.when(s > me)
        def _():
            @pl.when(me > 0)
            def _():
                sum_copy(s, q, True).wait_recv()
                sums[q, s] = sums[q, s] + arrived[s + 1, q]

            @pl.when((me > 0) | (k > 0))
            def _():
                sum_copy(s, q, True).start()

    def relay_down(k, q):
        @pl.when(k < me)
        def _():
            @pl.when(me < slots - 1)
            def _():
                sum_copy(k, q, False).wait_recv()
                sums[q, k] = sums[q, k] + arrived[k, q]

            @pl.when((me < slots - 1) | (k > 0))
            def _():
                sum_copy(k, q, False).start()

    for q in range(chunks):
        if q < chunks - 1:
            project(q, wq[:, q * width : (q + 1) * width])
        else:
            project(q, wkv[...])

        @pl.when(me == 0)
        def _():
            sum_copy(slots - 1, q, True).start()

        @pl.when(me == slots - 1)
        def _():
            sum_copy(0, q, False).start()

    steps = (slots - 1) * chunks
    paced = min(steps, 2 * half_pieces)

    def relay(i):
        k, q = i // chunks, i % chunks
        relay_up(k, q)
        relay_down(k, q)

        @pl.when(jnp.logical_not(edge) & (i < paced))
        def _():
            piece(i).start()

    each(steps, relay)

    def drain_sums(i):
        k, q = i // chunks, i % chunks

        @pl.when(slots - 1 - k > me)
        def _():
            sum_copy(slots - 1 - k, q, True).wait_send()

        @pl.when(k < me)
        def _():
            sum_copy(k, q, False).wait_send()

    @pl.when(edge)
    def _():
        each(steps, drain_sums)
        each(half_pieces, lambda i: piece(i).start())

    @pl.when(jnp.logical_not(edge))
    def _():
        each(2 * half_pieces, lambda i: piece(i).start(), paced)

    def settle(q):
        @pl.when(me > 0)
        def _():
            sum_copy(me, q, True).wait_recv()
            sums[q, me] = sums[q, me] + arrived[me + 1, q]

        @pl.when(me < slots - 1)
        def _():
            sum_copy(me, q, False).wait_recv()
            sums[q, me] = sums[q, me] + arrived[me, q]

    each(chunks, settle)

    qc, qs = qc_ref[...], qs_ref[...]
    for g in range(kv_heads):
        at = g * 2 * HD
        keys[g, past:, :] = turn(sums[chunks - 1, me, :, at : at + HD], qc, qs).astype(jnp.bfloat16)
        fresh[g] = sums[chunks - 1, me, :, at + HD : at + 2 * HD].astype(jnp.bfloat16)
    for h in range(heads):
        q, at = divmod(h * HD, width)
        queries[h * rows : (h + 1) * rows, :] = turn(
            sums[q, me, :, at : at + HD], qc, qs
        ).astype(jnp.bfloat16)

    def rotate_share(source):
        at_t = pl.multiple_of(source * share, share)
        tc, ts = tc_ref[pl.ds(at_t, share), :], ts_ref[pl.ds(at_t, share), :]

        def one(c):
            at_k = pl.multiple_of((source * NCH + c) * share, share)
            oc, os = oc_ref[pl.ds(c, 1), :], os_ref[pl.ds(c, 1), :]
            cos = tc * oc - ts * os
            sin = ts * oc + tc * os
            for g in range(kv_heads):
                at = g * 2 * HD
                x = blocks[source, c, :, at : at + HD].astype(jnp.float32)
                keys[g, pl.ds(at_k, share), :] = turn(x, cos, sin).astype(jnp.bfloat16)

        each(NCH, one)

    own_copy.wait()
    rotate_share(me)

    @pl.when(edge)
    def _():
        each(half_pieces, lambda i: piece(i).wait_send())
        each(2 * half_pieces, lambda i: piece(i).start(), half_pieces)

    def take(k):
        for g in range(kv_heads):
            block_copy(k, g, 0).wait_recv()
        rotate_share(lax.rem(me - k + slots, slots))

    each(slots, take, 1)

    block = 2 * rows
    span = 512
    factor = math.log2(math.e) / math.sqrt(HD)
    lower = lax.broadcasted_iota(jnp.int32, (block, rows), 0) % rows >= lax.broadcasted_iota(
        jnp.int32, (block, rows), 1
    )
    contract = (((1,), (1,)), ((), ()))

    def weigh(b):
        g = (b * 2) // sharing
        at = pl.ds(pl.multiple_of(b * block, block), block)
        q = queries[at, :]
        own = lax.dot_general(q, keys[g, past:, :], contract, preferred_element_type=jnp.float32)
        own = jnp.where(lower, own, -jnp.inf)
        top = own
        for j in range(past // span):
            s = lax.dot_general(
                q, keys[g, j * span : (j + 1) * span, :], contract,
                preferred_element_type=jnp.float32,
            )
            scores[:, j * span : (j + 1) * span] = s
            for k in range(span // HD):
                top = jnp.maximum(top, s[:, k * HD : (k + 1) * HD])
        top = jnp.max(top, axis=1, keepdims=True)
        w = jnp.exp2((own - top) * factor)
        total = w
        weights[at, past:] = w.astype(jnp.bfloat16)
        for j in range(past // span):
            w = jnp.exp2((scores[:, j * span : (j + 1) * span] - top) * factor)
            for k in range(span // HD):
                total = total + w[:, k * HD : (k + 1) * HD]
            weights[at, j * span : (j + 1) * span] = w.astype(jnp.bfloat16)
        totals[at, :] = total

    each(heads // 2, weigh)

    stack = sharing * rows
    some = NCH * share

    def mix(source, first):
        cols = pl.ds(pl.multiple_of(source * some, some), some)
        for g in range(kv_heads):
            at = slice(g * stack, (g + 1) * stack)
            v = blocks[source, :, :, (2 * g + 1) * HD : (2 * g + 2) * HD].reshape(some, HD)
            term = jnp.dot(weights[at, cols], v, preferred_element_type=jnp.float32)
            if first:
                mixed[at, :] = term + jnp.dot(
                    weights[at, past:], fresh[g], preferred_element_type=jnp.float32
                )
            else:
                mixed[at, :] = mixed[at, :] + term

    mix(me, True)

    def take_values(k):
        for g in range(kv_heads):
            block_copy(k, g, 1).wait_recv()
        mix(lax.rem(me - k + slots, slots), False)

    each(slots, take_values, 1)

    def finish(h):
        at = pl.ds(pl.multiple_of(h * rows, rows), rows)
        done = mixed[at, :] / jnp.sum(totals[at, :], axis=1, keepdims=True)
        out_ref[0, :, pl.ds(pl.multiple_of(h * HD, HD), HD)] = done.astype(out_ref.dtype)

    each(heads, finish)

    def drain(k):
        strip_copy(k).wait_send()
        for d in range(1, peers):
            spread_copy(k, d).wait_send()

    each(slots, drain, 1)
    each(2 * half_pieces, lambda i: piece(i).wait_send(), half_pieces)

    @pl.when(jnp.logical_not(edge))
    def _():
        each(steps, drain_sums)
        each(half_pieces, lambda i: piece(i).wait_send())


def per_device(hidden, query_weight, keyvalue_weight, block_store, block_ids, offsets, served):
    slots = lax.axis_size("store")
    peers = lax.axis_size("mp")
    me = lax.axis_index("store")
    rows, model = hidden.shape[1:]
    share, kv_cols = block_store.shape[1:]
    q_cols = query_weight.shape[1]
    heads = q_cols // HD
    kv_heads = kv_cols // (2 * HD)
    chunks = q_cols // kv_cols + 1
    depth = model // slots
    past = NCH * L
    sending = gather_blocks(block_ids, served, block_store)
    qc, qs = signed_tables(past + GAP + np.arange(rows))
    tc, ts = signed_tables(np.arange(L))
    oc, os = offset_tables(offsets[served[me]])
    vmem = pl.BlockSpec(memory_space=pltpu.VMEM)
    hbm = pl.BlockSpec(memory_space=pl.ANY)
    dma = pltpu.SemaphoreType.DMA
    return pl.pallas_call(
        functools.partial(serve_body, slots, peers, heads, kv_heads),
        out_shape=jax.ShapeDtypeStruct((1, rows, q_cols), jnp.bfloat16),
        in_specs=[vmem, hbm, hbm, hbm] + [vmem] * 6,
        out_specs=vmem,
        scratch_shapes=[
            pltpu.VMEM((slots, rows, depth), jnp.bfloat16),
            pltpu.VMEM(query_weight.shape, jnp.bfloat16),
            pltpu.VMEM(keyvalue_weight.shape, jnp.bfloat16),
            pltpu.VMEM((chunks, slots, rows, kv_cols), jnp.float32),
            pltpu.VMEM((slots + 1, chunks, rows, kv_cols), jnp.float32),
            pltpu.VMEM((slots, NCH, share, kv_cols), jnp.bfloat16),
            pltpu.VMEM((kv_heads, past + rows, HD), jnp.bfloat16),
            pltpu.VMEM((kv_heads, rows, HD), jnp.bfloat16),
            pltpu.VMEM((heads * rows, HD), jnp.bfloat16),
            pltpu.VMEM((2 * rows, past), jnp.float32),
            pltpu.VMEM((heads * rows, past + rows), jnp.bfloat16),
            pltpu.VMEM((heads * rows, HD), jnp.float32),
            pltpu.VMEM((heads * rows, HD), jnp.float32),
            dma((2,)),
            dma((1,)),
            dma((slots,)),
            dma((slots,)),
            dma((slots, peers)),
            dma((slots, peers)),
            dma((slots, 2 * kv_heads)),
            dma((slots, 2 * kv_heads)),
            dma((slots + 1, chunks)),
            dma((slots + 1, chunks)),
        ],
        compiler_params=pltpu.CompilerParams(
            vmem_limit_bytes=63 << 20, collective_id=0, has_side_effects=True
        ),
        name="serve",
    )(hidden, query_weight, keyvalue_weight, sending, qc, qs, tc, ts, oc, os)


def solution(mesh):
    in_specs = (
        P(("groups", "store"), None, None),
        P("store", "mp"),
        P("store", "mp"),
        P("groups", "store", "mp"),
        P("groups", None),
        P("groups", None),
        P("groups"),
    )
    out_specs = P(("groups", "store"), None, "mp")
    return jax.shard_map(
        per_device, mesh=mesh, in_specs=in_specs, out_specs=out_specs, check_vma=False
    )
```

```python
import functools
import math

import jax
import jax.numpy as jnp
import numpy as np
from jax import lax
from jax.experimental import pallas as pl
from jax.experimental.pallas import tpu as pltpu
from jax.sharding import PartitionSpec as P

HD = 128
HALF = HD // 2
NCH = 4
L = 1024
GAP = 64
BASE = 500000.0


def periods():
    inverse = np.exp(
        np.arange(HALF, dtype=np.float32) * np.float32(-2.0 * math.log(BASE) / HD)
    ).astype(np.float32)
    return np.floor(np.float32(2.0 * math.pi) / inverse + np.float32(0.5)).astype(np.float64)


def signed_tables(positions):
    period = periods()[None, :]
    angles = np.mod(np.asarray(positions, np.float64)[:, None], period) / period * (2.0 * math.pi)
    cos, sin = np.cos(angles), np.sin(angles)
    return (
        np.concatenate([cos, cos], axis=1).astype(np.float32),
        np.concatenate([-sin, sin], axis=1).astype(np.float32),
    )


def offset_tables(offsets):
    period = jnp.asarray(periods(), jnp.float32)[None, :]
    angles = jnp.mod(offsets.astype(jnp.float32)[:, None], period) / period * (2.0 * math.pi)
    cos, sin = jnp.cos(angles), jnp.sin(angles)
    return jnp.concatenate([cos, cos], axis=1), jnp.concatenate([-sin, sin], axis=1)


def gather_body(slots, ids_ref, served_ref, store_ref, out_ref, sems):
    copies = []
    for s in range(slots):
        request = served_ref[s]
        for c in range(NCH):
            copy = pltpu.make_async_copy(
                store_ref.at[ids_ref[request, c]], out_ref.at[s, c], sems.at[s, c]
            )
            copy.start()
            copies.append(copy)
    for copy in copies:
        copy.wait()


def gather_blocks(block_ids, served, block_store):
    slots = served.shape[0]
    return pl.pallas_call(
        functools.partial(gather_body, slots),
        grid_spec=pltpu.PrefetchScalarGridSpec(
            num_scalar_prefetch=2,
            grid=(),
            in_specs=[pl.BlockSpec(memory_space=pl.ANY)],
            out_specs=pl.BlockSpec(memory_space=pltpu.VMEM),
            scratch_shapes=[pltpu.SemaphoreType.DMA((slots, NCH))],
        ),
        out_shape=jax.ShapeDtypeStruct((slots, NCH) + block_store.shape[1:], block_store.dtype),
        compiler_params=pltpu.CompilerParams(vmem_limit_bytes=56 << 20),
        name="gather_blocks",
    )(block_ids, served, block_store)


def turn(x, cos, sin):
    return x * cos + pltpu.roll(x, HALF, 1) * sin


MESH = pl.DeviceIdType.MESH
ENDS, MIDDLE = 2, 2


def serve_body(
    slots, peers, heads, kv_heads,
    hidden_ref, wq_hbm, wkv_hbm, sending_ref, qc_ref, qs_ref, tc_ref, ts_ref, oc_ref, os_ref,
    out_ref,
    tokens, wq, wkv, sums, arrived, blocks, keys, fresh, queries, scores, weights, totals, mixed,
    load_sem, own_sem, a_send, a_recv, b_send, b_recv, k_send, k_recv, p_send, p_recv,
):
    me = lax.axis_index("store")
    part = lax.axis_index("mp")
    rows = hidden_ref.shape[1]
    depth = tokens.shape[2]
    chunks, _, _, width = sums.shape
    share = blocks.shape[2]
    sharing = heads // kv_heads
    past = NCH * L
    strip = rows // peers

    loads = [
        pltpu.make_async_copy(wq_hbm, wq, load_sem.at[0]),
        pltpu.make_async_copy(wkv_hbm, wkv, load_sem.at[1]),
    ]
    for load in loads:
        load.start()
    own_copy = pltpu.make_async_copy(sending_ref.at[me], blocks.at[me], own_sem.at[0])
    own_copy.start()

    barrier = pltpu.get_barrier_semaphore()
    for k in range(1, slots):
        pl.semaphore_signal(
            barrier, inc=1, device_id={"store": lax.rem(me + k, slots)}, device_id_type=MESH
        )
    for k in range(1, peers):
        pl.semaphore_signal(
            barrier, inc=1, device_id={"mp": lax.rem(part + k, peers)}, device_id_type=MESH
        )
    pl.semaphore_wait(barrier, slots + peers - 2)

    def strip_copy(k):
        to = lax.rem(me + k, slots)
        mine = pl.ds(pl.multiple_of(part * strip, strip), strip)
        return pltpu.make_async_remote_copy(
            src_ref=hidden_ref.at[0, mine, pl.ds(pl.multiple_of(to * depth, depth), depth)],
            dst_ref=tokens.at[me, mine, :],
            send_sem=a_send.at[k],
            recv_sem=a_recv.at[k],
            device_id={"store": to},
            device_id_type=MESH,
        )

    def spread_copy(k, d):
        source = lax.rem(me - k + slots, slots)
        mine = pl.ds(pl.multiple_of(part * strip, strip), strip)
        return pltpu.make_async_remote_copy(
            src_ref=tokens.at[source, mine, :],
            dst_ref=tokens.at[source, mine, :],
            send_sem=b_send.at[k, d],
            recv_sem=b_recv.at[k, d],
            device_id={"mp": lax.rem(part + d, peers)},
            device_id_type=MESH,
        )

    def block_copy(k, g, v):
        to = lax.rem(me + k, slots)
        cols = pl.ds(pl.multiple_of((2 * g + v) * HD, HD), HD)
        return pltpu.make_async_remote_copy(
            src_ref=sending_ref.at[to, :, :, cols],
            dst_ref=blocks.at[me, :, :, cols],
            send_sem=k_send.at[k, 2 * g + v],
            recv_sem=k_recv.at[k, 2 * g + v],
            device_id={"store": to},
            device_id_type=MESH,
        )

    half_pieces = (slots - 1) * kv_heads

    def piece(i):
        v, r = i // half_pieces, i % half_pieces
        return block_copy(1 + r // kv_heads, r % kv_heads, v)

    edge = (me == 0) | (me == slots - 1)

    def sum_copy(s, q, up):
        index = s + 1 if up else s
        return pltpu.make_async_remote_copy(
            src_ref=sums.at[q, s],
            dst_ref=arrived.at[index, q],
            send_sem=p_send.at[index, q],
            recv_sem=p_recv.at[index, q],
            device_id={"store": lax.rem(me + 1, slots) if up else lax.rem(me + slots - 1, slots)},
            device_id_type=MESH,
        )

    def each(count, body, first=0):
        def step(i, carry):
            body(i)
            return carry

        lax.fori_loop(first, count, step, 0)

    each(slots, lambda k: strip_copy(k).start(), 1)
    ends_first, middle_first = ENDS * half_pieces, MIDDLE * half_pieces

    @pl.when(edge)
    def _():
        each(ends_first, lambda i: piece(i).start())

    @pl.when(jnp.logical_not(edge))
    def _():
        each(middle_first, lambda i: piece(i).start())

    tokens[me] = hidden_ref[0, :, pl.ds(pl.multiple_of(me * depth, depth), depth)]

    def spread(k):
        strip_copy(k).wait_recv()
        for d in range(1, peers):
            spread_copy(k, d).start()

    each(slots, spread, 1)

    def spread_wait(k):
        for d in range(1, peers):
            spread_copy(k, d).wait_recv()

    each(slots, spread_wait, 1)
    for load in loads:
        load.wait()

    group = 4 if slots % 4 == 0 else 1

    def project(q, panel):
        def some(i):
            t = tokens[pl.ds(i * group, group)].reshape(group * rows, depth)
            sums[q, pl.ds(i * group, group)] = jnp.dot(
                t, panel, preferred_element_type=jnp.float32
            ).reshape(group, rows, width)

        each(slots // group, some)

    def relay_up(k, q):
        s = slots - 1 - k

        @pl.when(s > me)
        def _():
            @pl.when(me > 0)
            def _():
                sum_copy(s, q, True).wait_recv()
                sums[q, s] = sums[q, s] + arrived[s + 1, q]

            @pl.when((me > 0) | (k > 0))
            def _():
                sum_copy(s, q, True).start()

    def relay_down(k, q):
        @pl.when(k < me)
        def _():
            @pl.when(me < slots - 1)
            def _():
                sum_copy(k, q, False).wait_recv()
                sums[q, k] = sums[q, k] + arrived[k, q]

            @pl.when((me < slots - 1) | (k > 0))
            def _():
                sum_copy(k, q, False).start()

    for q in range(chunks):
        if q < chunks - 1:
            project(q, wq[:, q * width : (q + 1) * width])
        else:
            project(q, wkv[...])

        @pl.when(me == 0)
        def _():
            sum_copy(slots - 1, q, True).start()

        @pl.when(me == slots - 1)
        def _():
            sum_copy(0, q, False).start()

    steps = (slots - 1) * chunks
    paced = min(steps, 2 * half_pieces)

    def relay(i):
        k, q = i // chunks, i % chunks
        relay_up(k, q)
        relay_down(k, q)

        @pl.when(jnp.logical_not(edge) & (i + middle_first < paced))
        def _():
            piece(i + middle_first).start()

    each(steps, relay)

    def drain_sums(i):
        k, q = i // chunks, i % chunks

        @pl.when(slots - 1 - k > me)
        def _():
            sum_copy(slots - 1 - k, q, True).wait_send()

        @pl.when(k < me)
        def _():
            sum_copy(k, q, False).wait_send()

    @pl.when(edge)
    def _():
        each(2 * half_pieces, lambda i: piece(i).start(), ends_first)

    @pl.when(jnp.logical_not(edge))
    def _():
        each(2 * half_pieces, lambda i: piece(i).start(), paced)

    def settle(q):
        @pl.when(me > 0)
        def _():
            sum_copy(me, q, True).wait_recv()
            sums[q, me] = sums[q, me] + arrived[me + 1, q]

        @pl.when(me < slots - 1)
        def _():
            sum_copy(me, q, False).wait_recv()
            sums[q, me] = sums[q, me] + arrived[me, q]

    each(chunks, settle)

    qc, qs = qc_ref[...], qs_ref[...]
    for g in range(kv_heads):
        at = g * 2 * HD
        keys[g, past:, :] = turn(sums[chunks - 1, me, :, at : at + HD], qc, qs).astype(jnp.bfloat16)
        fresh[g] = sums[chunks - 1, me, :, at + HD : at + 2 * HD].astype(jnp.bfloat16)
    for h in range(heads):
        q, at = divmod(h * HD, width)
        queries[h * rows : (h + 1) * rows, :] = turn(
            sums[q, me, :, at : at + HD], qc, qs
        ).astype(jnp.bfloat16)

    def rotate_share(source):
        at_t = pl.multiple_of(source * share, share)
        tc, ts = tc_ref[pl.ds(at_t, share), :], ts_ref[pl.ds(at_t, share), :]

        def one(c):
            at_k = pl.multiple_of((source * NCH + c) * share, share)
            oc, os = oc_ref[pl.ds(c, 1), :], os_ref[pl.ds(c, 1), :]
            cos = tc * oc - ts * os
            sin = ts * oc + tc * os
            for g in range(kv_heads):
                at = g * 2 * HD
                x = blocks[source, c, :, at : at + HD].astype(jnp.float32)
                keys[g, pl.ds(at_k, share), :] = turn(x, cos, sin).astype(jnp.bfloat16)

        each(NCH, one)

    own_copy.wait()
    rotate_share(me)

    def take(k):
        for g in range(kv_heads):
            block_copy(k, g, 0).wait_recv()
        rotate_share(lax.rem(me - k + slots, slots))

    each(slots, take, 1)

    block = 2 * rows
    span = 512
    factor = math.log2(math.e) / math.sqrt(HD)
    lower = lax.broadcasted_iota(jnp.int32, (block, rows), 0) % rows >= lax.broadcasted_iota(
        jnp.int32, (block, rows), 1
    )
    contract = (((1,), (1,)), ((), ()))

    def weigh(b):
        g = (b * 2) // sharing
        at = pl.ds(pl.multiple_of(b * block, block), block)
        q = queries[at, :]
        own = lax.dot_general(q, keys[g, past:, :], contract, preferred_element_type=jnp.float32)
        own = jnp.where(lower, own, -jnp.inf)
        top = own
        for j in range(past // span):
            s = lax.dot_general(
                q, keys[g, j * span : (j + 1) * span, :], contract,
                preferred_element_type=jnp.float32,
            )
            scores[:, j * span : (j + 1) * span] = s
            for k in range(span // HD):
                top = jnp.maximum(top, s[:, k * HD : (k + 1) * HD])
        top = jnp.max(top, axis=1, keepdims=True)
        w = jnp.exp2((own - top) * factor)
        total = w
        weights[at, past:] = w.astype(jnp.bfloat16)
        for j in range(past // span):
            w = jnp.exp2((scores[:, j * span : (j + 1) * span] - top) * factor)
            for k in range(span // HD):
                total = total + w[:, k * HD : (k + 1) * HD]
            weights[at, j * span : (j + 1) * span] = w.astype(jnp.bfloat16)
        totals[at, :] = total

    each(heads // 2, weigh)

    stack = sharing * rows
    some = NCH * share

    def mix(source, first):
        cols = pl.ds(pl.multiple_of(source * some, some), some)
        for g in range(kv_heads):
            at = slice(g * stack, (g + 1) * stack)
            v = blocks[source, :, :, (2 * g + 1) * HD : (2 * g + 2) * HD].reshape(some, HD)
            term = jnp.dot(weights[at, cols], v, preferred_element_type=jnp.float32)
            if first:
                mixed[at, :] = term + jnp.dot(
                    weights[at, past:], fresh[g], preferred_element_type=jnp.float32
                )
            else:
                mixed[at, :] = mixed[at, :] + term

    mix(me, True)

    def take_values(k):
        for g in range(kv_heads):
            block_copy(k, g, 1).wait_recv()
        mix(lax.rem(me - k + slots, slots), False)

    each(slots, take_values, 1)

    def finish(h):
        at = pl.ds(pl.multiple_of(h * rows, rows), rows)
        done = mixed[at, :] / jnp.sum(totals[at, :], axis=1, keepdims=True)
        out_ref[0, :, pl.ds(pl.multiple_of(h * HD, HD), HD)] = done.astype(out_ref.dtype)

    each(heads, finish)

    def drain(k):
        strip_copy(k).wait_send()
        for d in range(1, peers):
            spread_copy(k, d).wait_send()

    each(slots, drain, 1)
    each(2 * half_pieces, lambda i: piece(i).wait_send())
    each(steps, drain_sums)


def per_device(hidden, query_weight, keyvalue_weight, block_store, block_ids, offsets, served):
    slots = lax.axis_size("store")
    peers = lax.axis_size("mp")
    me = lax.axis_index("store")
    rows, model = hidden.shape[1:]
    share, kv_cols = block_store.shape[1:]
    q_cols = query_weight.shape[1]
    heads = q_cols // HD
    kv_heads = kv_cols // (2 * HD)
    chunks = q_cols // kv_cols + 1
    depth = model // slots
    past = NCH * L
    sending = gather_blocks(block_ids, served, block_store)
    qc, qs = signed_tables(past + GAP + np.arange(rows))
    tc, ts = signed_tables(np.arange(L))
    oc, os = offset_tables(offsets[served[me]])
    vmem = pl.BlockSpec(memory_space=pltpu.VMEM)
    hbm = pl.BlockSpec(memory_space=pl.ANY)
    dma = pltpu.SemaphoreType.DMA
    return pl.pallas_call(
        functools.partial(serve_body, slots, peers, heads, kv_heads),
        out_shape=jax.ShapeDtypeStruct((1, rows, q_cols), jnp.bfloat16),
        in_specs=[vmem, hbm, hbm, hbm] + [vmem] * 6,
        out_specs=vmem,
        scratch_shapes=[
            pltpu.VMEM((slots, rows, depth), jnp.bfloat16),
            pltpu.VMEM(query_weight.shape, jnp.bfloat16),
            pltpu.VMEM(keyvalue_weight.shape, jnp.bfloat16),
            pltpu.VMEM((chunks, slots, rows, kv_cols), jnp.float32),
            pltpu.VMEM((slots + 1, chunks, rows, kv_cols), jnp.float32),
            pltpu.VMEM((slots, NCH, share, kv_cols), jnp.bfloat16),
            pltpu.VMEM((kv_heads, past + rows, HD), jnp.bfloat16),
            pltpu.VMEM((kv_heads, rows, HD), jnp.bfloat16),
            pltpu.VMEM((heads * rows, HD), jnp.bfloat16),
            pltpu.VMEM((2 * rows, past), jnp.float32),
            pltpu.VMEM((heads * rows, past + rows), jnp.bfloat16),
            pltpu.VMEM((heads * rows, HD), jnp.float32),
            pltpu.VMEM((heads * rows, HD), jnp.float32),
            dma((2,)),
            dma((1,)),
            dma((slots,)),
            dma((slots,)),
            dma((slots, peers)),
            dma((slots, peers)),
            dma((slots, 2 * kv_heads)),
            dma((slots, 2 * kv_heads)),
            dma((slots + 1, chunks)),
            dma((slots + 1, chunks)),
        ],
        compiler_params=pltpu.CompilerParams(
            vmem_limit_bytes=63 << 20, collective_id=0, has_side_effects=True
        ),
        name="serve",
    )(hidden, query_weight, keyvalue_weight, sending, qc, qs, tc, ts, oc, os)


def solution(mesh):
    in_specs = (
        P(("groups", "store"), None, None),
        P("store", "mp"),
        P("store", "mp"),
        P("groups", "store", "mp"),
        P("groups", None),
        P("groups", None),
        P("groups"),
    )
    out_specs = P(("groups", "store"), None, "mp")
    return jax.shard_map(
        per_device, mesh=mesh, in_specs=in_specs, out_specs=out_specs, check_vma=False
    )
```
